32 devices in a mesh: groups: 2 (over x), seq: 16 (over z, y, core).
Axes of the slice: x: 2, y: 2, z: 4, core: 2. Of those that a mesh axis runs over, the one named last changes fastest.
Arguments:
- queries: bfloat16 [16384, 4096], P(('groups', 'seq')), parts along dimension 0, may hold values from -80 to 80
- keys: bfloat16 [16384, 1024], P(('groups', 'seq')), parts along dimension 0, may hold values from -4 to 4
- values: bfloat16 [16384, 1024], P(('groups', 'seq')), parts along dimension 0, may hold values from -6 to 6
- doc_start: int32 [16384], P(('groups', 'seq')), parts along dimension 0, may hold values from 0 to 8191, as said below
- block_list: int32 [128, 8], P(('groups', 'seq')), parts along dimension 0, may hold values from -1 to 63, as said below
Outputs:
- attended: bfloat16 [16384, 4096], P(('groups', 'seq')), parts along dimension 0
The draws below stay inside these ranges and needn't reach their ends.
There are 2 independent parts, one for each index of `groups`. The reference program is written for one: setup_inputs(seed, part) draws one part's arguments, and reference() takes and returns one part's arrays. A program takes and returns all parts, laid end to end along the dimension named above; each array names one. Nothing has to cross between parts.
Inputs may be any that keep to these rules, and one draw needn't show every extreme that they name: doc_start[i] <= i and i - doc_start[i] < 2048; doc_start never falls and changes only to i itself where a new document begins at i; some document holds exactly 2048 tokens; the window's last token begins a document of its own. `block_list`: row q names distinct key blocks, filled slots first and -1 after them; its first entry is q itself; every entry e satisfies q - 16 <= e <= q and lies at or after the block that holds doc_start of position q * 128; some row fills all 8 slots.
All inputs are finite; a program needn't handle non-finite values.
Results may differ from the reference program's by a relative error of at most 0.0045.
Values may be sent and summed in bfloat16 or wider, within the bound.
No kernel may reach another device: no remote copies, remote signals or barrier semaphores. Data moves between devices by JAX's collectives and lax.ppermute only.
A program may use at most 128 MiB of HBM per device.

```python
import jax
import jax.numpy as jnp
from jax import lax

HEADS = 32
KV_HEADS = 8
HEAD_DIM = 128
BLOCK = 128
NNZ = 8
TOKENS = 8192
DOC_MOST = 2048


def document_starts(key):
    doc_total = 8 * TOKENS // DOC_MOST + 2
    lengths = jax.random.randint(jax.random.fold_in(key, 11), (doc_total,), DOC_MOST // 8, DOC_MOST + 1)
    chosen = jax.random.randint(jax.random.fold_in(key, 12), (), 0, TOKENS // DOC_MOST - 1)
    lengths = jnp.where(jnp.arange(doc_total) == chosen, DOC_MOST, lengths).astype(jnp.int32)
    doc_ends = jnp.cumsum(lengths)
    begins = doc_ends - lengths
    places = jnp.arange(TOKENS, dtype=jnp.int32)
    doc_index = jnp.sum((doc_ends[None, :] <= places[:, None]).astype(jnp.int32), axis=1)
    found = begins[doc_index].astype(jnp.int32)
    return jnp.where(places == TOKENS - 1, places, found).astype(jnp.int32)


def draw_doc_start(key, part):
    return document_starts(key)


def draw_block_list(key, part):
    starts = document_starts(key)
    block_total = TOKENS // BLOCK
    reach_blocks = DOC_MOST // BLOCK
    lowest = starts[::BLOCK] // BLOCK
    row_ids = jnp.arange(block_total, dtype=jnp.int32)
    offsets = jnp.arange(reach_blocks + 1, dtype=jnp.int32)
    candidate = row_ids[:, None] - offsets[None, :]
    usable = candidate >= lowest[:, None]
    noise_bits = jax.random.randint(jax.random.fold_in(key, 13), (block_total, reach_blocks + 1), 0, 1 << 20)
    ranking = noise_bits * (reach_blocks + 1) + offsets[None, :]
    ranking = ranking + jnp.where(usable, 1 << 26, 0) + jnp.where(offsets[None, :] == 0, 1 << 28, 0)
    picked_score, picked = lax.top_k(ranking, NNZ)
    picked_usable = jnp.take_along_axis(usable, picked, axis=1)
    return jnp.where(picked_usable, row_ids[:, None] - picked, -1).astype(jnp.int32)


def key_normals(key):
    drawn = jax.random.normal(jax.random.fold_in(key, 21), (TOKENS, KV_HEADS * HEAD_DIM), jnp.float32)
    return jnp.clip(drawn, -4.0, 4.0)


def draw_keys(key, part):
    normal_rows = key_normals(key)
    return normal_rows.astype(jnp.bfloat16)


def draw_queries(key, part):
    drawn = jax.random.normal(jax.random.fold_in(key, 22), (TOKENS, HEADS * HEAD_DIM), jnp.float32)
    normal_rows = jnp.clip(drawn, -4.0, 4.0)
    return normal_rows.astype(jnp.bfloat16)


def block_levels(own_key, shape, cuts, smallest, largest):
    loudness, own = 1.0, jax.random.fold_in(own_key, 6)
    for dim, shards_of in cuts:
        heights = jnp.exp(jax.random.uniform(jax.random.fold_in(own, dim), (shards_of,), jnp.float32, smallest / len(cuts), largest / len(cuts)))
        loudness = loudness * jnp.repeat(heights, shape[dim] // shards_of).reshape([-1 if axis == dim else 1 for axis in range(len(shape))])
    return loudness


def gaussian(key, extent, deviation, reach, shards=(), kind=jnp.bfloat16):
    level = block_levels(key, extent, shards, -0.22, 0.18) if shards else 1.0
    values = jax.random.normal(key, extent, jnp.float32) * deviation * level
    return jnp.minimum(jnp.maximum(values, -reach), reach).astype(kind)


def setup_inputs(seed: int = 0, part: int = 0) -> dict:
    streams_of = jax.random.split(jax.random.key(seed), 6)
    own_keys = jax.random.split(jax.random.fold_in(streams_of[5], part), 6)
    return {
        "queries": draw_queries(jax.random.fold_in(jax.random.fold_in(streams_of[5], part), 71), part),
        "keys": draw_keys(jax.random.fold_in(jax.random.fold_in(streams_of[5], part), 71), part),
        "values": gaussian(own_keys[2], (TOKENS, KV_HEADS * HEAD_DIM), 1.0, 6.0, ((0, 16),)),
        "doc_start": draw_doc_start(jax.random.fold_in(jax.random.fold_in(streams_of[5], part), 71), part),
        "block_list": draw_block_list(jax.random.fold_in(jax.random.fold_in(streams_of[5], part), 71), part),
    }


NEG_BIG = -1.0e30


def reference(queries, keys, values, doc_start, block_list):
    block_total = TOKENS // BLOCK
    group_size = HEADS // KV_HEADS
    key_blocks = keys.reshape(block_total, BLOCK, KV_HEADS, HEAD_DIM)
    value_blocks = values.reshape(block_total, BLOCK, KV_HEADS, HEAD_DIM)
    query_blocks = queries.reshape(block_total, BLOCK, KV_HEADS, group_size, HEAD_DIM)
    start_blocks = doc_start.reshape(block_total, BLOCK)
    offsets = jnp.arange(BLOCK, dtype=jnp.int32)

    def one_block(block_id):
        entries = block_list[block_id]
        safe_ids = jnp.maximum(entries, 0)
        key_rows = jnp.take(key_blocks, safe_ids, axis=0).reshape(-1, KV_HEADS, HEAD_DIM).astype(jnp.float32)
        value_rows = jnp.take(value_blocks, safe_ids, axis=0).reshape(-1, KV_HEADS, HEAD_DIM).astype(jnp.float32)
        key_pos = (entries[:, None] * BLOCK + offsets[None, :]).reshape(-1)
        key_live = jnp.repeat(entries >= 0, BLOCK)
        positions = block_id * BLOCK + offsets
        starts = start_blocks[block_id]
        allowed = key_live[None, :] & (key_pos[None, :] >= starts[:, None]) & (key_pos[None, :] <= positions[:, None])
        scores = jnp.einsum("qhgd,khd->hgqk", query_blocks[block_id].astype(jnp.float32), key_rows) * (HEAD_DIM ** -0.5)
        row_top = jnp.max(jnp.where(allowed, scores, NEG_BIG), axis=-1)
        weights = jnp.where(allowed, jnp.exp(scores - row_top[..., None]), 0.0)
        row_total = jnp.sum(weights, axis=-1)
        rounded = lax.optimization_barrier(weights.astype(jnp.bfloat16)).astype(jnp.float32)
        mixed_sum = jnp.einsum("hgqk,khd->qhgd", rounded, value_rows)
        result = mixed_sum / jnp.transpose(row_total, (2, 0, 1))[..., None]
        return result.reshape(BLOCK, HEADS * HEAD_DIM).astype(jnp.bfloat16)

    attended = lax.map(one_block, jnp.arange(block_total, dtype=jnp.int32))
    return attended.reshape(TOKENS, HEADS * HEAD_DIM)
```

```python
import functools

import jax
import jax.numpy as jnp
from jax import lax
from jax.experimental import pallas as pl
from jax.experimental.pallas import tpu as pltpu
from jax.sharding import PartitionSpec as P

HEAD_DIM = 128
BLOCK = 128
GROUP = 4
SHARDS = 5
PAIR = 2 * BLOCK
CHUNKS = (8,)
ROWS = 256
NEG_BIG = -1e30
LOG2E = 1.4426950408889634
SCALE = HEAD_DIM**-0.5 * LOG2E


def kernel(heads, aliased, table, bias, queries, *refs):
    sources = refs[:SHARDS]
    out, key_window, value_window, sems = refs[SHARDS + aliased :]
    step = pl.program_id(0)
    shard_rows = sources[0].shape[1]
    slots = bias.shape[1] // BLOCK
    blocks = bias.shape[0]

    def copies(head, slot):
        columns = pl.ds(pl.multiple_of(head * HEAD_DIM, HEAD_DIM), HEAD_DIM)
        made = []
        for n, source in enumerate(sources):
            rows = pl.ds(n * shard_rows, shard_rows)
            for m, window in enumerate((key_window, value_window)):
                made.append(
                    pltpu.make_async_copy(
                        source.at[m, :, columns], window.at[slot, rows, :], sems.at[slot, 2 * n + m]
                    )
                )
        return made

    slot = lax.rem(step, 2)

    @pl.when(step == 0)
    def _():
        for copy in copies(0, 0):
            copy.start()

    @pl.when(step + 1 < heads)
    def _():
        for copy in copies(step + 1, 1 - slot):
            copy.start()

    for copy in copies(step, slot):
        copy.wait()

    row_ids = lax.broadcasted_iota(jnp.int32, (BLOCK, BLOCK), 0)
    column_ids = lax.broadcasted_iota(jnp.int32, (BLOCK, BLOCK), 1)
    eye = (row_ids == column_ids).astype(jnp.bfloat16)
    per_pass = ROWS // BLOCK
    picker = jnp.concatenate([eye] * per_pass, 0)
    ones = jnp.ones((PAIR, HEAD_DIM), jnp.bfloat16)

    def block_rows(block_id, carry):
        first = pl.multiple_of(block_id * BLOCK, BLOCK)

        def pair_of(window, p):
            parts = []
            for j in (2 * p, 2 * p + 1):
                start = pl.multiple_of(table[block_id * slots + j] * BLOCK, BLOCK)
                parts.append(window[slot, pl.ds(start, BLOCK), :])
            return jnp.concatenate(parts, 0)

        for h0 in range(0, GROUP, per_pass):
            heads_now = range(h0, h0 + per_pass)
            rows = jnp.concatenate(
                [queries[pl.ds(first, BLOCK), h * HEAD_DIM : (h + 1) * HEAD_DIM] for h in heads_now], 0
            )
            rows = jnp.concatenate([rows, picker], 1)
            scores = []
            for p in range(slots // 2):
                masked_keys = jnp.concatenate(
                    [pair_of(key_window, p), bias[block_id, p * PAIR : (p + 1) * PAIR, :]], 1
                )
                scores.append(
                    lax.dot_general(
                        rows, masked_keys, (((1,), (1,)), ((), ())), preferred_element_type=jnp.float32
                    )
                )
            top = jnp.max(functools.reduce(jnp.maximum, scores), axis=1, keepdims=True)
            mixed = None
            for p in range(slots // 2):
                weights = jnp.exp2((scores[p] - top) * SCALE).astype(jnp.bfloat16)
                term = jnp.dot(
                    weights,
                    jnp.concatenate([pair_of(value_window, p), ones], 1),
                    preferred_element_type=jnp.float32,
                )
                mixed = term if mixed is None else mixed + term
            result = (mixed[:, :HEAD_DIM] / mixed[:, HEAD_DIM:]).astype(jnp.bfloat16)
            for n, h in enumerate(heads_now):
                out[pl.ds(first, BLOCK), h * HEAD_DIM : (h + 1) * HEAD_DIM] = result[
                    n * BLOCK : (n + 1) * BLOCK
                ]
        return carry

    lax.fori_loop(0, blocks, block_rows, 0)


def attend(table, bias, queries, sources, previous, first, heads):
    tokens, width = queries.shape
    group_width = GROUP * HEAD_DIM
    aliased = 0 if previous is None else 1
    anywhere = pl.BlockSpec(memory_space=pl.ANY)
    columns = pl.BlockSpec((tokens, group_width), lambda i, t: (0, first + i))
    work = tokens * GROUP * heads * bias.shape[1] * HEAD_DIM
    return pl.pallas_call(
        functools.partial(kernel, heads, aliased),
        grid_spec=pltpu.PrefetchScalarGridSpec(
            num_scalar_prefetch=1,
            grid=(heads,),
            in_specs=[pl.BlockSpec(bias.shape, lambda i, t: (0, 0, 0)), columns]
            + [anywhere] * (SHARDS + aliased),
            out_specs=columns,
            scratch_shapes=[
                pltpu.VMEM((2, SHARDS * tokens, HEAD_DIM), jnp.bfloat16),
                pltpu.VMEM((2, SHARDS * tokens, HEAD_DIM), jnp.bfloat16),
                pltpu.SemaphoreType.DMA((2, 2 * SHARDS)),
            ],
        ),
        out_shape=jax.ShapeDtypeStruct((tokens, width), jnp.bfloat16),
        input_output_aliases={3 + SHARDS: 0} if aliased else {},
        cost_estimate=pl.CostEstimate(
            flops=8 * work, bytes_accessed=4 * tokens * width, transcendentals=work // HEAD_DIM
        ),
        compiler_params=pltpu.CompilerParams(vmem_limit_bytes=32 << 20),
        name="attend",
    )(table, bias, queries, *sources, *(() if previous is None else (previous,)))


def masks(doc_start, block_list, shard):
    blocks = block_list.shape[0]
    offsets = jnp.arange(BLOCK, dtype=jnp.int32)
    starts = doc_start.reshape(blocks, 1, 1, BLOCK)
    places = ((shard * blocks + jnp.arange(blocks, dtype=jnp.int32))[:, None] * BLOCK + offsets)[
        :, None, None, :
    ]
    key_places = block_list[:, :, None, None] * BLOCK + offsets[:, None]
    allowed = (block_list >= 0)[:, :, None, None] & (key_places >= starts) & (key_places <= places)
    bias = jnp.where(allowed, 0.0, NEG_BIG).astype(jnp.bfloat16)
    return bias.reshape(blocks, -1, BLOCK)


def window_table(block_list, shard):
    blocks = block_list.shape[0]
    core = shard % 2
    entries = jnp.maximum(block_list, 0)
    behind = shard - entries // blocks
    nearest, third = jnp.where(core == 0, 4, 3), jnp.where(core == 0, 3, 4)
    place = jnp.where(behind == 1, nearest, 0)
    place = jnp.where(behind == 2, 1, place)
    place = jnp.where(behind == 3, third, place)
    place = jnp.where(behind == 4, 2, place)
    rows = place * blocks + entries % blocks
    return jnp.where(block_list >= 0, rows, 0).astype(jnp.int32).reshape(-1)


def local(queries, keys, values, doc_start, block_list):
    shard = lax.axis_index("seq")
    devices = range(lax.axis_size("seq"))
    core, row = shard % 2, (shard // 2) % 2
    two_back = [(i - 4, i) for i in devices if i >= 4]
    one_back = [(i ^ 2, i) for i in devices if i >= 2]
    sibling = [(i ^ 1, i) for i in devices]
    bias = masks(doc_start, block_list, shard)
    table = window_table(block_list, shard)
    out = None
    first = 0
    for heads in CHUNKS:
        columns = slice(first * HEAD_DIM, (first + heads) * HEAD_DIM)
        own = jnp.stack([keys[:, columns], values[:, columns]])
        from_z = lax.ppermute(own, "seq", two_back)
        from_y = lax.ppermute(jnp.where(row == 0, own, from_z), "seq", one_back)
        twin_x = lax.ppermute(jnp.where(core == 0, own, from_z), "seq", sibling)
        twin_y = lax.ppermute(from_y, "seq", sibling)
        out = attend(table, bias, queries, (own, from_y, from_z, twin_x, twin_y), out, first, heads)
        first += heads
    return out


def solution(mesh):
    shards = P(("groups", "seq"))
    return jax.shard_map(
        local,
        mesh=mesh,
        in_specs=(shards,) * 5,
        out_specs=shards,
        check_vma=False,
    )
```

```python
import functools

import jax
import jax.numpy as jnp
from jax import lax
from jax.experimental import pallas as pl
from jax.experimental.pallas import tpu as pltpu
from jax.sharding import PartitionSpec as P


HEAD_DIM = 128
BLOCK = 128
GROUP = 4
SHARDS = 5
PAIR = 2 * BLOCK
CHUNKS = (1, 2, 2, 2, 1)
SUBLANES = 16
VMEM_LIMIT = 32 << 20
NEG_BIG = -1e30
LOG2E = 1.4426950408889634
SCALE = HEAD_DIM**-0.5 * LOG2E


def kernel(aliased, table, bias, queries, *refs):
    sources = refs[:SHARDS]
    out, key_window, value_window, scores, weights, tops = refs[SHARDS + aliased :]
    step = pl.program_id(0)
    blocks, listed = bias.shape[0], bias.shape[1]
    slots = listed // BLOCK
    shard_rows = sources[0].shape[2]
    width = GROUP * HEAD_DIM
    for m, window in enumerate((key_window, value_window)):
        for n, source in enumerate(sources):
            window[n * shard_rows : (n + 1) * shard_rows, :] = source[step, m]

    row_ids = lax.broadcasted_iota(jnp.int32, (BLOCK, BLOCK), 0)
    column_ids = lax.broadcasted_iota(jnp.int32, (BLOCK, BLOCK), 1)
    eye = (row_ids == column_ids).astype(jnp.bfloat16)
    picker = jnp.concatenate([eye] * GROUP, 0)
    ones = jnp.ones((SUBLANES, listed), jnp.bfloat16)

    def parts(window, block_id):
        made = []
        for j in range(slots):
            start = pl.multiple_of(table[block_id * slots + j] * BLOCK, BLOCK)
            made.append(window[pl.ds(start, BLOCK), :])
        return made

    def score(block_id, b):
        rows = slice(block_id * BLOCK, (block_id + 1) * BLOCK)
        stacked = [queries[rows, h * HEAD_DIM : (h + 1) * HEAD_DIM] for h in range(GROUP)]
        found = lax.dot_general(
            jnp.concatenate([jnp.concatenate(parts(key_window, block_id), 0), bias[block_id]], 1),
            jnp.concatenate([jnp.concatenate(stacked, 0), picker], 1),
            (((1,), (1,)), ((), ())),
            preferred_element_type=jnp.float32,
        )
        scores[b] = found
        tops[b] = jnp.max(found.reshape(-1, 8, width), axis=0)

    def soften(b):
        top = jnp.max(tops[b], axis=0, keepdims=True)
        for p in range(0, listed, PAIR):
            rows = slice(p, p + PAIR)
            weights[b, rows] = jnp.exp2((scores[b, rows] - top) * SCALE).astype(jnp.bfloat16)

    def mix(block_id, b):
        mixed = jnp.dot(
            jnp.concatenate([jnp.concatenate(parts(value_window, block_id), 1), ones], 0),
            weights[b],
            preferred_element_type=jnp.float32,
        )
        result = mixed[:HEAD_DIM] * (1.0 / mixed[HEAD_DIM : HEAD_DIM + 1])
        rows = slice(block_id * BLOCK, (block_id + 1) * BLOCK)
        for h in range(GROUP):
            columns = slice(h * HEAD_DIM, (h + 1) * HEAD_DIM)
            out[rows, columns] = result[:, h * BLOCK : (h + 1) * BLOCK].T.astype(jnp.bfloat16)

    for t in range(blocks + 2):
        if t < blocks:
            score(t, t % 2)
        if 0 <= t - 1 < blocks:
            soften((t - 1) % 2)
        if 0 <= t - 2 < blocks:
            mix(t - 2, (t - 2) % 2)


def attend(table, bias, queries, sources, previous, first, heads):
    tokens, width = queries.shape
    listed = bias.shape[1]
    group_width = GROUP * HEAD_DIM
    aliased = 0 if previous is None else 1
    near = pl.BlockSpec(memory_space=pltpu.VMEM)
    columns = pl.BlockSpec((tokens, group_width), lambda i, t: (0, first + i))
    work = tokens * GROUP * heads * listed * HEAD_DIM
    return pl.pallas_call(
        functools.partial(kernel, aliased),
        grid_spec=pltpu.PrefetchScalarGridSpec(
            num_scalar_prefetch=1,
            grid=(heads,),
            in_specs=[near, columns] + [near] * SHARDS + [pl.BlockSpec(memory_space=pl.ANY)] * aliased,
            out_specs=columns,
            scratch_shapes=[
                pltpu.VMEM((SHARDS * tokens, HEAD_DIM), jnp.bfloat16),
                pltpu.VMEM((SHARDS * tokens, HEAD_DIM), jnp.bfloat16),
                pltpu.VMEM((2, listed, group_width), jnp.float32),
                pltpu.VMEM((2, listed, group_width), jnp.bfloat16),
                pltpu.VMEM((2, 8, group_width), jnp.float32),
            ],
        ),
        out_shape=jax.ShapeDtypeStruct((tokens, width), jnp.bfloat16),
        input_output_aliases={3 + SHARDS: 0} if aliased else {},
        cost_estimate=pl.CostEstimate(
            flops=8 * work, bytes_accessed=4 * tokens * width, transcendentals=work // HEAD_DIM
        ),
        compiler_params=pltpu.CompilerParams(vmem_limit_bytes=VMEM_LIMIT),
        name="attend",
    )(table, bias, pltpu.with_memory_space_constraint(queries, pltpu.HBM), *sources, *(() if previous is None else (previous,)))


def plan_kernel(place, listed, starts, bias, table):
    shard = place[0]
    blocks, slots = listed.shape
    core = shard % 2
    shape = (BLOCK, BLOCK)
    key_offsets = lax.broadcasted_iota(jnp.int32, shape, 0)
    row_offsets = lax.broadcasted_iota(jnp.int32, shape, 1)
    for b in range(blocks):
        places = (shard * blocks + b) * BLOCK + row_offsets
        begins = jnp.broadcast_to(starts[b : b + 1, :], shape)
        for j in range(slots):
            entry = listed[b, j]
            key_places = entry * BLOCK + key_offsets
            allowed = (key_places >= begins) & (key_places <= places) & (entry >= 0)
            bias[b, j * BLOCK : (j + 1) * BLOCK, :] = jnp.where(allowed, 0.0, NEG_BIG).astype(jnp.bfloat16)
            known = jnp.maximum(entry, 0)
            shard_of = lax.div(known, blocks)
            behind = shard - shard_of
            where = jnp.where(behind == 1, 4 - core, 0)
            where = jnp.where(behind == 2, 1, where)
            where = jnp.where(behind == 3, 3 + core, where)
            where = jnp.where(behind == 4, 2, where)
            where = jnp.where(entry >= 0, where, 0)
            table[b * slots + j] = where * blocks + known - shard_of * blocks


def plan(doc_start, block_list, shard):
    blocks, slots = block_list.shape
    scalars, vectors = pl.BlockSpec(memory_space=pltpu.SMEM), pl.BlockSpec(memory_space=pltpu.VMEM)
    return pl.pallas_call(
        plan_kernel,
        in_specs=[scalars, scalars, vectors],
        out_specs=[vectors, scalars],
        out_shape=[
            jax.ShapeDtypeStruct((blocks, slots * BLOCK, BLOCK), jnp.bfloat16),
            jax.ShapeDtypeStruct((blocks * slots,), jnp.int32),
        ],
        compiler_params=pltpu.CompilerParams(vmem_limit_bytes=VMEM_LIMIT),
        name="plan",
    )(shard.reshape(1), block_list, doc_start.reshape(blocks, BLOCK))


def pack_kernel(spans, keys, values, *outs):
    for (first, heads), out in zip(spans, outs):
        for h in range(heads):
            columns = slice((first + h) * HEAD_DIM, (first + h + 1) * HEAD_DIM)
            out[h, 0] = keys[:, columns]
            for b in range(0, keys.shape[0], BLOCK):
                out[h, 1, b : b + BLOCK, :] = values[b : b + BLOCK, columns].T


def pack(keys, values, spans):
    tokens = keys.shape[0]
    width = sum(heads for _, heads in spans) * HEAD_DIM
    taken = pl.BlockSpec((tokens, width if spans[0][0] == 0 else keys.shape[1]), lambda i: (0, 0))
    shapes = [(heads, 2, tokens, HEAD_DIM) for _, heads in spans]
    return pl.pallas_call(
        functools.partial(pack_kernel, spans),
        grid=(1,),
        in_specs=[taken, taken],
        out_specs=[pl.BlockSpec(shape, lambda i: (0, 0, 0, 0)) for shape in shapes],
        out_shape=[jax.ShapeDtypeStruct(shape, keys.dtype) for shape in shapes],
        compiler_params=pltpu.CompilerParams(vmem_limit_bytes=VMEM_LIMIT),
        name="pack",
    )(*(pltpu.with_memory_space_constraint(x, pltpu.HBM) for x in (keys, values)))


def routed(queries, keys, values, doc_start, block_list):
    shard = lax.axis_index("seq")
    devices = range(lax.axis_size("seq"))
    core, row = shard % 2, (shard // 2) % 2
    two_back = [(i - 4, i) for i in devices if i >= 4]
    one_back = [(i ^ 2, i) for i in devices if i >= 2]
    sibling = [(i ^ 1, i) for i in devices]
    bias, table = plan(doc_start, block_list, shard)
    firsts = [sum(CHUNKS[:n]) for n in range(len(CHUNKS))]
    spans = list(zip(firsts, CHUNKS))
    owns = pack(keys, values, spans[:1]) + pack(keys, values, spans[1:])
    from_z = []
    for n in range(len(CHUNKS)):
        from_z.append(lax.ppermute(owns[n], "seq", two_back))
    out = None
    for n, heads in enumerate(CHUNKS):
        own, back = owns[n], from_z[n]
        from_y = lax.ppermute(jnp.where(row == 0, own, back), "seq", one_back)
        twin_x = lax.ppermute(jnp.where(core == 0, own, back), "seq", sibling)
        twin_y = lax.ppermute(from_y, "seq", sibling)
        out = attend(table, bias, queries, (own, from_y, back, twin_x, twin_y), out, firsts[n], heads)
    return out


def solution(mesh):
    shards = P(("groups", "seq"))
    return jax.shard_map(
        routed,
        mesh=mesh,
        in_specs=(shards,) * 5,
        out_specs=shards,
        check_vma=False,
    )
```

```python
import functools

import jax
import jax.numpy as jnp
from jax import lax
from jax.experimental import pallas as pl
from jax.experimental.pallas import tpu as pltpu
from jax.sharding import PartitionSpec as P


HEAD_DIM = 128
BLOCK = 128
GROUP = 4
SHARDS = 5
PAIR = 2 * BLOCK
CHUNKS = (1, 2, 2, 2, 1)
SUBLANES = 16
VMEM_LIMIT = 32 << 20
NEG_BIG = -1e30
LOG2E = 1.4426950408889634
SCALE = HEAD_DIM**-0.5 * LOG2E


def kernel(first, earlier, table, bias, queries, *refs):
    sources, done = refs[:SHARDS], refs[SHARDS : SHARDS + len(earlier)]
    out, key_window, value_window, scores, weights, tops, *rest = refs[SHARDS + len(earlier) :]
    step = pl.program_id(0)
    blocks, listed = bias.shape[0], bias.shape[1]
    slots = listed // BLOCK
    shard_rows = sources[0].shape[2]
    width = GROUP * HEAD_DIM
    for m, window in enumerate((key_window, value_window)):
        for n, source in enumerate(sources):
            window[n * shard_rows : (n + 1) * shard_rows, :] = source[step, m]

    def columns_of(head):
        return pl.ds(pl.multiple_of(head * width, width), width)

    staged, moves = out, []
    if earlier:
        staged, early_sems, own_sems = rest
        for n, (start, part) in enumerate(zip(earlier, done)):
            columns = slice(start * width, start * width + part.shape[1])
            moves.append(pltpu.make_async_copy(part, out.at[:, columns], early_sems.at[n]))

        @pl.when(step == 0)
        def _():
            for move in moves:
                move.start()

    def own_move(block_id):
        rows = pl.ds(block_id * BLOCK, BLOCK)
        return pltpu.make_async_copy(
            staged.at[rows, columns_of(step)],
            out.at[rows, columns_of(first + step)],
            own_sems.at[step, block_id],
        )

    row_ids = lax.broadcasted_iota(jnp.int32, (BLOCK, BLOCK), 0)
    column_ids = lax.broadcasted_iota(jnp.int32, (BLOCK, BLOCK), 1)
    eye = (row_ids == column_ids).astype(jnp.bfloat16)
    picker = jnp.concatenate([eye] * GROUP, 0)
    ones = jnp.ones((SUBLANES, listed), jnp.bfloat16)

    def parts(window, block_id):
        made = []
        for j in range(slots):
            start = pl.multiple_of(table[block_id * slots + j] * BLOCK, BLOCK)
            made.append(window[pl.ds(start, BLOCK), :])
        return made

    def score(block_id, b):
        rows = slice(block_id * BLOCK, (block_id + 1) * BLOCK)
        stacked = []
        for h in range(GROUP):
            column = pl.multiple_of((first + step) * width + h * HEAD_DIM, HEAD_DIM)
            stacked.append(queries[rows, pl.ds(column, HEAD_DIM)])
        found = lax.dot_general(
            jnp.concatenate([jnp.concatenate(parts(key_window, block_id), 0), bias[block_id]], 1),
            jnp.concatenate([jnp.concatenate(stacked, 0), picker], 1),
            (((1,), (1,)), ((), ())),
            preferred_element_type=jnp.float32,
        )
        scores[b] = found
        tops[b] = jnp.max(found.reshape(-1, 8, width), axis=0)

    def soften(b):
        top = jnp.max(tops[b], axis=0, keepdims=True)
        for p in range(0, listed, PAIR):
            rows = slice(p, p + PAIR)
            weights[b, rows] = jnp.exp2((scores[b, rows] - top) * SCALE).astype(jnp.bfloat16)

    def mix(block_id, b):
        mixed = jnp.dot(
            jnp.concatenate([jnp.concatenate(parts(value_window, block_id), 1), ones], 0),
            weights[b],
            preferred_element_type=jnp.float32,
        )
        result = mixed[:HEAD_DIM] * (1.0 / mixed[HEAD_DIM : HEAD_DIM + 1])
        rows = slice(block_id * BLOCK, (block_id + 1) * BLOCK)
        for h in range(GROUP):
            columns = pl.ds(pl.multiple_of(step * width + h * HEAD_DIM, HEAD_DIM), HEAD_DIM)
            staged[rows, columns] = result[:, h * BLOCK : (h + 1) * BLOCK].T.astype(jnp.bfloat16)

    for t in range(blocks + 2):
        if t < blocks:
            score(t, t % 2)
        if 0 <= t - 1 < blocks:
            soften((t - 1) % 2)
        if 0 <= t - 2 < blocks:
            mix(t - 2, (t - 2) % 2)
            if earlier:
                own_move(t - 2).start()
    if earlier:
        for b in range(blocks):
            own_move(b).wait()

        @pl.when(step + 1 == pl.num_programs(0))
        def _():
            for move in moves:
                move.wait()


def attend(table, bias, queries, sources, earlier, first, heads):
    tokens, width = queries.shape
    blocks, listed = bias.shape[0], bias.shape[1]
    group_width = GROUP * HEAD_DIM
    near = pl.BlockSpec(memory_space=pltpu.VMEM)
    work = tokens * GROUP * heads * listed * HEAD_DIM
    scratch = [
        pltpu.VMEM((SHARDS * tokens, HEAD_DIM), jnp.bfloat16),
        pltpu.VMEM((SHARDS * tokens, HEAD_DIM), jnp.bfloat16),
        pltpu.VMEM((2, listed, group_width), jnp.float32),
        pltpu.VMEM((2, listed, group_width), jnp.bfloat16),
        pltpu.VMEM((2, 8, group_width), jnp.float32),
    ]
    if earlier:
        scratch += [
            pltpu.VMEM((tokens, heads * group_width), jnp.bfloat16),
            pltpu.SemaphoreType.DMA((len(earlier),)),
            pltpu.SemaphoreType.DMA((heads, blocks)),
        ]
    else:
        width = heads * group_width
    return pl.pallas_call(
        functools.partial(kernel, first, tuple(start for start, _ in earlier)),
        grid_spec=pltpu.PrefetchScalarGridSpec(
            num_scalar_prefetch=1,
            grid=(heads,),
            in_specs=[near] * (2 + SHARDS + len(earlier)),
            out_specs=pl.BlockSpec(memory_space=pltpu.HBM) if earlier else near,
            scratch_shapes=scratch,
        ),
        out_shape=jax.ShapeDtypeStruct((tokens, width), jnp.bfloat16),
        cost_estimate=pl.CostEstimate(
            flops=8 * work, bytes_accessed=4 * tokens * width, transcendentals=work // HEAD_DIM
        ),
        compiler_params=pltpu.CompilerParams(vmem_limit_bytes=VMEM_LIMIT),
        name="attend",
    )(table, bias, queries, *sources, *(part for _, part in earlier))


def plan_kernel(place, listed, starts, queries, bias, table, near_queries, sem):
    fetch = pltpu.make_async_copy(queries, near_queries, sem)
    fetch.start()
    shard = place[0]
    blocks, slots = listed.shape
    core = shard % 2
    shape = (BLOCK, BLOCK)
    key_offsets = lax.broadcasted_iota(jnp.int32, shape, 0)
    row_offsets = lax.broadcasted_iota(jnp.int32, shape, 1)
    for b in range(blocks):
        places = (shard * blocks + b) * BLOCK + row_offsets
        begins = jnp.broadcast_to(starts[b : b + 1, :], shape)
        for j in range(slots):
            entry = listed[b, j]
            key_places = entry * BLOCK + key_offsets
            allowed = (key_places >= begins) & (key_places <= places) & (entry >= 0)
            bias[b, j * BLOCK : (j + 1) * BLOCK, :] = jnp.where(allowed, 0.0, NEG_BIG).astype(jnp.bfloat16)
            known = jnp.maximum(entry, 0)
            shard_of = lax.div(known, blocks)
            behind = shard - shard_of
            where = jnp.where(behind == 1, 4 - core, 0)
            where = jnp.where(behind == 2, 1, where)
            where = jnp.where(behind == 3, 3 + core, where)
            where = jnp.where(behind == 4, 2, where)
            where = jnp.where(entry >= 0, where, 0)
            table[b * slots + j] = where * blocks + known - shard_of * blocks
    fetch.wait()


def plan(doc_start, block_list, queries, shard):
    blocks, slots = block_list.shape
    scalars, vectors = pl.BlockSpec(memory_space=pltpu.SMEM), pl.BlockSpec(memory_space=pltpu.VMEM)
    return pl.pallas_call(
        plan_kernel,
        in_specs=[scalars, scalars, vectors, pl.BlockSpec(memory_space=pltpu.HBM)],
        out_specs=[vectors, scalars, vectors],
        out_shape=[
            jax.ShapeDtypeStruct((blocks, slots * BLOCK, BLOCK), jnp.bfloat16),
            jax.ShapeDtypeStruct((blocks * slots,), jnp.int32),
            jax.ShapeDtypeStruct(queries.shape, queries.dtype),
        ],
        scratch_shapes=[pltpu.SemaphoreType.DMA],
        compiler_params=pltpu.CompilerParams(vmem_limit_bytes=VMEM_LIMIT),
        name="plan",
    )(shard.reshape(1), block_list, doc_start.reshape(blocks, BLOCK), pltpu.with_memory_space_constraint(queries, pltpu.HBM))


def pack_kernel(spans, keys, values, *outs):
    for (first, heads), out in zip(spans, outs):
        for h in range(heads):
            columns = slice((first + h) * HEAD_DIM, (first + h + 1) * HEAD_DIM)
            out[h, 0] = keys[:, columns]
            for b in range(0, keys.shape[0], BLOCK):
                out[h, 1, b : b + BLOCK, :] = values[b : b + BLOCK, columns].T


def pack(keys, values, spans):
    tokens = keys.shape[0]
    width = sum(heads for _, heads in spans) * HEAD_DIM
    taken = pl.BlockSpec((tokens, width if spans[0][0] == 0 else keys.shape[1]), lambda i: (0, 0))
    shapes = [(heads, 2, tokens, HEAD_DIM) for _, heads in spans]
    return pl.pallas_call(
        functools.partial(pack_kernel, spans),
        grid=(1,),
        in_specs=[taken, taken],
        out_specs=[pl.BlockSpec(shape, lambda i: (0, 0, 0, 0)) for shape in shapes],
        out_shape=[jax.ShapeDtypeStruct(shape, keys.dtype) for shape in shapes],
        compiler_params=pltpu.CompilerParams(vmem_limit_bytes=VMEM_LIMIT),
        name="pack",
    )(*(pltpu.with_memory_space_constraint(x, pltpu.HBM) for x in (keys, values)))


def routed(queries, keys, values, doc_start, block_list):
    shard = lax.axis_index("seq")
    devices = range(lax.axis_size("seq"))
    core, row = shard % 2, (shard // 2) % 2
    two_back = [(i - 4, i) for i in devices if i >= 4]
    one_back = [(i ^ 2, i) for i in devices if i >= 2]
    sibling = [(i ^ 1, i) for i in devices]
    bias, table, queries = plan(doc_start, block_list, queries, shard)
    firsts = [sum(CHUNKS[:n]) for n in range(len(CHUNKS))]
    spans = list(zip(firsts, CHUNKS))
    owns = pack(keys, values, spans[:1]) + pack(keys, values, spans[1:])
    from_z = []
    for n in range(len(CHUNKS)):
        from_z.append(lax.ppermute(owns[n], "seq", two_back))
    parts = []
    for n, heads in enumerate(CHUNKS):
        own, back = owns[n], from_z[n]
        from_y = lax.ppermute(jnp.where(row == 0, own, back), "seq", one_back)
        twin_x = lax.ppermute(jnp.where(core == 0, own, back), "seq", sibling)
        twin_y = lax.ppermute(from_y, "seq", sibling)
        sources = (own, from_y, back, twin_x, twin_y)
        earlier = parts if n + 1 == len(CHUNKS) else []
        parts.append((firsts[n], attend(table, bias, queries, sources, earlier, firsts[n], heads)))
    return parts[-1][1]


def solution(mesh):
    shards = P(("groups", "seq"))
    return jax.shard_map(
        routed,
        mesh=mesh,
        in_specs=(shards,) * 5,
        out_specs=shards,
        check_vma=False,
    )
```
